32 devices in a mesh: dp: 16 (over z, y, core), tensor: 2 (over x).
Axes of the slice: x: 2, y: 2, z: 4, core: 2. Of those that a mesh axis runs over, the one named last changes fastest.
Arguments:
- inputs: bfloat16 [9216, 8192], P('dp', 'tensor'), may hold values from -6 to 6
- out_grads: bfloat16 [9216, 11264], P('dp', 'tensor'), may hold values from -600 to 600
- basis: bfloat16 [8192, 512], P('dp', 'tensor'), may hold values from -40 to 40
- weight: bfloat16 [8192, 11264], P('dp', 'tensor'), may hold values from -0.099609375 to 0.099609375
- first_moment: float32 [512, 11264], P('dp', 'tensor'), may hold values from -0.9 to 0.9
- second_moment: float32 [512, 11264], P('dp', 'tensor'), may hold values from 0.01 to 1
Outputs:
- new_weight: bfloat16 [8192, 11264], P('dp', 'tensor')
- new_first: float32 [512, 11264], P('dp', 'tensor')
- new_second: float32 [512, 11264], P('dp', 'tensor')
The draws below stay inside these ranges and needn't reach their ends.
All inputs are finite; a program needn't handle non-finite values.
Results may differ from the reference program's by a relative error of at most 0.0087.
Values may be sent and summed in bfloat16 or wider, within the bound.
A program may use at most 64 MiB of HBM per device.

```python
import math
import jax
import jax.numpy as jnp
from jax import lax

D = 8192
FW = 11264
R = 512
TOKENS = 9216


def rising(key, count):
    place = jnp.arange(count, dtype=jnp.float32) / count
    jitter = jnp.exp(jax.random.uniform(key, (count,), jnp.float32, -0.6931, 0.6931))
    return 10.0 ** place * jitter


def draw_basis(key, part):
    first_key, second_key = jax.random.split(jax.random.fold_in(key, 17))
    entries = jnp.clip(jax.random.normal(first_key, (D, R), jnp.float32), -2.0, 2.0)
    scales = rising(second_key, R)
    return (entries * scales[None, :]).astype(jnp.bfloat16)


def draw_out_grads(key, part):
    keys = jax.random.split(jax.random.fold_in(key, 29), 3)
    token_scales = jnp.exp(jax.random.uniform(keys[0], (TOKENS,), jnp.float32, 0.0, 2.3026))
    column_scales = rising(keys[1], FW)
    entries = jnp.clip(jax.random.normal(keys[2], (TOKENS, FW), jnp.float32), -3.0, 3.0)
    return (entries * token_scales[:, None] * column_scales[None, :]).astype(jnp.bfloat16)


def steps_of(rng, extent, cuts, least, high):
    def one(axis_at, parts):
        steps = jax.random.uniform(jax.random.fold_in(jax.random.fold_in(rng, 6), axis_at), (parts,), jnp.float32, least / len(cuts), high / len(cuts))
        return jnp.repeat(jnp.exp(steps), extent[axis_at] // parts).reshape((-1,) + (1,) * (len(extent) - axis_at - 1))

    factor_of = one(*cuts[0])
    for cut in cuts[1:]:
        factor_of = factor_of * one(*cut)
    return factor_of


def noise(stream_key, shape, spread, bound, cuts=(), kind=jnp.bfloat16):
    drawn = spread * jax.random.normal(stream_key, shape, jnp.float32)
    if cuts:
        drawn = drawn * steps_of(stream_key, shape, cuts, -0.22, 0.18)
    return jnp.clip(drawn, -bound, bound).astype(kind)


def setup_inputs(seed: int = 0) -> dict:
    key_of = jax.random.split(jax.random.key(seed), 7)
    inputs = noise(key_of[0], (TOKENS, D), 1.0, 6.0, ((0, 16), (1, 2)))
    out_grads = draw_out_grads(jax.random.fold_in(key_of[6], 71), 0)
    basis = draw_basis(jax.random.fold_in(key_of[6], 71), 0)
    weight = noise(key_of[3], (D, FW), 0.02, 0.099609375, ((0, 16), (1, 2)))
    first_moment = noise(key_of[4], (R, FW), 0.15, 0.9, ((0, 16), (1, 2)), jnp.float32)
    second_moment = jnp.clip(jnp.exp(math.log(1.0) - 4.6051702 * jax.random.uniform(key_of[5], (R, FW), jnp.float32) ** steps_of(key_of[5], (R, FW), ((0, 16), (1, 2)), -0.2, 0.2)), 0.01, 1.0)
    return {"inputs": inputs, "out_grads": out_grads, "basis": basis, "weight": weight, "first_moment": first_moment, "second_moment": second_moment}


beta_one = 0.9
beta_two = 0.999
adam_eps = 1e-08
corr_one = 1.0 - 0.9 ** 10
corr_two = 1.0 - 0.999 ** 10
step_size = 0.002
decay_keep = 0.99

def adam_update(lowrank, square, first_moment, second_moment):
    bound_norm = math.sqrt(R * FW)
    factor = jnp.minimum(1.0, bound_norm / (jnp.sqrt(square) + 1e-06))
    clipped = lowrank * factor
    first = beta_one * first_moment + (1.0 - beta_one) * clipped
    second = beta_two * second_moment + (1.0 - beta_two) * clipped * clipped
    update = (first / corr_one / (jnp.sqrt(second / corr_two) + adam_eps)).astype(jnp.bfloat16)
    return (first, second, update)

def reference(inputs, out_grads, basis, weight, first_moment, second_moment):
    projected = jnp.dot(inputs, basis, preferred_element_type=jnp.float32).astype(jnp.bfloat16)
    lowrank = lax.dot_general(projected, out_grads, (((0,), (0,)), ((), ())), preferred_element_type=jnp.float32)
    square = jnp.sum(lowrank * lowrank)
    first, second, update = adam_update(lowrank, square, first_moment, second_moment)
    delta = jnp.dot(basis, update, preferred_element_type=jnp.float32)
    new_weight = (decay_keep * weight.astype(jnp.float32) - step_size * delta).astype(jnp.bfloat16)
    return (new_weight, first, second)
```

```python
import functools
import math

import jax
import jax.numpy as jnp
from jax import lax
from jax.experimental import pallas as pl
from jax.experimental.pallas import tpu as pltpu
from jax.sharding import PartitionSpec as P

beta_one = 0.9
beta_two = 0.999
adam_eps = 1e-08
corr_one = 1.0 - 0.9**10
corr_two = 1.0 - 0.999**10
step_size = 0.002
decay_keep = 0.99

MESH = pl.DeviceIdType.MESH
ANY = pl.BlockSpec(memory_space=pl.ANY)
VMEM = pl.BlockSpec(memory_space=pltpu.VMEM)


def factors(dp):
    c = 2 if dp % 2 == 0 else 1
    y = 2 if (dp // c) % 2 == 0 else 1
    return dp // (c * y), y, c


def near_first(z):
    return sorted(range(1, z), key=lambda k: (min(k, z - k), k))


class Place:
    def __init__(self, dims, tensor):
        self.dims, self.tensor = dims, tensor
        d = lax.axis_index("dp")
        _, ny, nc = dims
        self.z, self.y, self.c = d // (ny * nc), (d // nc) % ny, d % nc
        self.t = lax.axis_index("tensor")

    def unit(self, k=0, j=0, i=0):
        nz, ny, nc = self.dims
        z = lax.rem(self.z + k + nz, nz) if k else self.z
        y = lax.rem(self.y + j + ny, ny) if j else self.y
        c = lax.rem(self.c + i + nc, nc) if i else self.c
        return (z * ny + y) * nc + c

    def peer(self, k=0, j=0, i=0, s=0):
        t = lax.rem(self.t + s, self.tensor) if s else self.t
        return (self.unit(k, j, i), t)

    def peers(self, tensor=True):
        nz, ny, nc = self.dims
        out = [self.peer(k=k) for k in range(1, nz)]
        out += [self.peer(j=j) for j in range(1, ny)]
        out += [self.peer(i=i) for i in range(1, nc)]
        if tensor:
            out += [self.peer(s=s) for s in range(1, self.tensor)]
        return out


def greet(peers):
    barrier = pltpu.get_barrier_semaphore()
    for p in peers:
        pl.semaphore_signal(barrier, inc=1, device_id=p, device_id_type=MESH)
    pl.semaphore_wait(barrier, len(peers))


def send(src, dst, sems, slot, peer):
    copy = pltpu.make_async_remote_copy(
        src_ref=src,
        dst_ref=dst,
        send_sem=sems.at[0, slot],
        recv_sem=sems.at[1, slot],
        device_id=peer,
        device_id_type=MESH,
    )
    copy.start()
    return copy


def gather(at, own, full, sems, base=0):
    nz, ny, nc = at.dims
    slot = [base]
    pending = []

    def go(k, j, i, src_unit, src):
        copy = send(src, full.at[src_unit], sems, slot[0], at.peer(k, j, i))
        slot[0] += 1
        pending.append(copy)
        return copy

    order = near_first(nz)
    across = {k: go(k, 0, 0, at.unit(), own) for k in order}
    sides, cores = {}, []
    for k in [0] + order:
        if k:
            across[k].wait_recv()
        u = at.unit(-k)
        src = full.at[u] if k else own
        for j in range(1, ny):
            sides[k, j] = go(0, j, 0, u, src)
        for i in range(1, nc):
            cores.append(go(0, 0, i, u, src))
    for k in [0] + order:
        for j in range(1, ny):
            sides[k, j].wait_recv()
            u = at.unit(-k, -j)
            for i in range(1, nc):
                cores.append(go(0, 0, i, u, full.at[u]))
    for copy in cores:
        copy.wait_recv()
    for copy in pending:
        copy.wait_send()


def basis_kernel(dims, tensor, own_ref, back_ref, full, back, sems, local):
    at = Place(dims, tensor)
    dp = math.prod(dims)
    greet(at.peers())
    mine = pltpu.make_async_copy(own_ref, full.at[at.unit()], local.at[0])
    mine_back = pltpu.make_async_copy(back_ref, back.at[at.t], local.at[1])
    mine.start()
    mine_back.start()
    gather(at, own_ref, full, sems)
    backs = [
        send(back_ref, back.at[at.t], sems, dp - 1 + s - 1, at.peer(s=s))
        for s in range(1, tensor)
    ]
    for copy in backs:
        copy.wait()
    mine.wait()
    mine_back.wait()


def gather_basis(moved, basis, dims, tensor):
    dp = math.prod(dims)
    count = dp - 1 + tensor - 1
    return pl.pallas_call(
        functools.partial(basis_kernel, dims, tensor),
        out_shape=(
            jax.ShapeDtypeStruct((dp,) + moved.shape, moved.dtype),
            jax.ShapeDtypeStruct((tensor,) + basis.shape, basis.dtype),
        ),
        in_specs=[ANY, ANY],
        out_specs=(ANY, ANY),
        scratch_shapes=[
            pltpu.SemaphoreType.DMA((2, count)),
            pltpu.SemaphoreType.DMA((2,)),
        ],
        compiler_params=pltpu.CompilerParams(collective_id=0, has_side_effects=True),
        name="gather_basis",
    )(moved, basis)


def project_kernel(tensor, chunks, in_ref, basis_ref, out_ref, own, sent, got, sems):
    me = lax.axis_index("tensor")
    d = lax.axis_index("dp")
    peers = [(d, lax.rem(me + s, tensor)) for s in range(1, tensor)]
    greet(peers)
    tokens = in_ref.shape[0] // chunks
    width = basis_ref.shape[2]
    copies = []
    for a in range(chunks):
        rows = pl.ds(a * tokens, tokens)
        for h in range(tensor):
            part = jnp.dot(in_ref[rows, :], basis_ref[h], preferred_element_type=jnp.float32)
            own[rows, h * width : (h + 1) * width] = part
            sent[rows, h * width : (h + 1) * width] = part.astype(jnp.bfloat16)
        for s in range(1, tensor):
            copies.append(
                send(
                    sent.at[rows],
                    got.at[s - 1, rows],
                    sems,
                    a * (tensor - 1) + s - 1,
                    peers[s - 1],
                )
            )
    for a in range(chunks):
        rows = pl.ds(a * tokens, tokens)
        total = own[rows, :]
        for s in range(1, tensor):
            copies[a * (tensor - 1) + s - 1].wait_recv()
            total = total + got[s - 1, rows, :].astype(jnp.float32)
        out_ref[rows, :] = total.astype(jnp.bfloat16)
    for copy in copies:
        copy.wait_send()


def project(inputs, basis, tensor):
    tokens = inputs.shape[0]
    rank = basis.shape[0] * basis.shape[2]
    chunks = 2
    return pl.pallas_call(
        functools.partial(project_kernel, tensor, chunks),
        out_shape=jax.ShapeDtypeStruct((tokens, rank), jnp.bfloat16),
        in_specs=[VMEM, VMEM],
        out_specs=VMEM,
        scratch_shapes=[
            pltpu.VMEM((tokens, rank), jnp.float32),
            pltpu.VMEM((tokens, rank), jnp.bfloat16),
            pltpu.VMEM((max(tensor - 1, 1), tokens, rank), jnp.bfloat16),
            pltpu.SemaphoreType.DMA((2, chunks * max(tensor - 1, 1))),
        ],
        compiler_params=pltpu.CompilerParams(collective_id=1, has_side_effects=True),
        name="project",
    )(inputs, basis)


def step_kernel(
    dims, tensor, bound_norm, part, m_ref, v_ref,
    first_ref, second_ref, full,
    r1, r2, r3, s1, s2, keep, upd, norm, sems, gather_sems, norm_sems, local,
):
    at = Place(dims, tensor)
    nz, ny, nc = dims
    f32 = jnp.float32
    greet(at.peers())

    order = near_first(nz)[::-1] + [0]
    slot = 0
    first_copies, second_copies, third_copies = {}, {}, {}
    for k in order:
        for j in [*range(1, ny), 0]:
            for i in range(1, nc):
                first_copies[k, j, i] = send(
                    part.at[at.unit(k, j, i)], r1.at[k, j, i - 1], sems, slot, at.peer(i=i)
                )
                slot += 1

    def over_cores(k, j):
        total = part[at.unit(k, j)].astype(f32)
        for i in range(1, nc):
            first_copies[k, j, i].wait_recv()
            total = total + r1[k, j, i - 1].astype(f32)
        return total

    def over_sides(k):
        total = keep[k]
        for j in range(1, ny):
            second_copies[k, j].wait_recv()
            total = total + r2[k, j - 1].astype(f32)
        return total

    def pass_on(k):
        nonlocal slot
        if k == 0:
            return
        s2[k - 1] = over_sides(k).astype(jnp.bfloat16)
        third_copies[k] = send(s2.at[k - 1], r3.at[k - 1], sems, slot, at.peer(k=k))
        slot += 1

    before = None
    for k in order:
        for j in range(1, ny):
            s1[k, j - 1] = over_cores(k, j).astype(jnp.bfloat16)
            second_copies[k, j] = send(s1.at[k, j - 1], r2.at[k, j - 1], sems, slot, at.peer(j=j))
            slot += 1
        keep[k] = over_cores(k, 0)
        if before is not None:
            pass_on(before)
        before = k
    total = over_sides(0)
    for k in order[:-1]:
        third_copies[k].wait_recv()
        total = total + r3[k - 1].astype(f32)
    keep[0] = total

    lanes = norm.shape[-1]
    rows, columns = total.shape
    squares = jnp.sum(total * total, axis=0, keepdims=True)
    folded = squares[:, :lanes]
    for a in range(1, columns // lanes):
        folded = folded + squares[:, a * lanes : (a + 1) * lanes]
    tally = jnp.broadcast_to(folded, (8, lanes))
    norm_copies, place = [], 0
    for count, axis in ((nc, "i"), (ny, "j"), (tensor, "s"), (nz, "k")):
        if count == 1:
            continue
        base = place
        norm[base] = tally
        copies = []
        for step in range(1, count):
            copies.append(
                send(norm.at[base], norm.at[base + step], norm_sems, base + step, at.peer(**{axis: step}))
            )
        for step in range(1, count):
            copies[step - 1].wait_recv()
            tally = tally + norm[base + step]
        norm_copies += copies
        place += count
    square = jnp.sum(tally[0:1, :], axis=1, keepdims=True)

    factor = jnp.minimum(1.0, bound_norm / (jnp.sqrt(square) + 1e-06))
    clipped = keep[0] * factor
    first = beta_one * m_ref[...] + (1.0 - beta_one) * clipped
    second = beta_two * v_ref[...] + (1.0 - beta_two) * clipped * clipped
    first_ref[...] = first
    second_ref[...] = second
    upd[...] = (first / corr_one / (jnp.sqrt(second / corr_two) + adam_eps)).astype(jnp.bfloat16)

    mine = pltpu.make_async_copy(upd, full.at[at.unit()], local)
    mine.start()
    gather(at, upd, full, gather_sems)
    mine.wait()
    for group in (first_copies, second_copies, third_copies):
        for copy in group.values():
            copy.wait_send()
    for copy in norm_copies:
        copy.wait_send()


def reduce_step(part, first_moment, second_moment, dims, tensor, bound_norm):
    dp, rows, columns = part.shape
    nz, ny, nc = dims
    bf16, f32 = jnp.bfloat16, jnp.float32
    sends = nz * ny * (nc - 1) + nz * (ny - 1) + nz - 1
    tallies = sum(n for n in (nz, ny, nc, tensor) if n > 1)
    at_least = lambda n: max(n, 1)
    return pl.pallas_call(
        functools.partial(step_kernel, dims, tensor, bound_norm),
        out_shape=(
            jax.ShapeDtypeStruct((rows, columns), f32),
            jax.ShapeDtypeStruct((rows, columns), f32),
            jax.ShapeDtypeStruct((dp, rows, columns), bf16),
        ),
        in_specs=[VMEM, VMEM, VMEM],
        out_specs=(VMEM, VMEM, ANY),
        scratch_shapes=[
            pltpu.VMEM((nz, ny, at_least(nc - 1), rows, columns), bf16),
            pltpu.VMEM((nz, at_least(ny - 1), rows, columns), bf16),
            pltpu.VMEM((at_least(nz - 1), rows, columns), bf16),
            pltpu.VMEM((nz, at_least(ny - 1), rows, columns), bf16),
            pltpu.VMEM((at_least(nz - 1), rows, columns), bf16),
            pltpu.VMEM((nz, rows, columns), f32),
            pltpu.VMEM((rows, columns), bf16),
            pltpu.VMEM((at_least(tallies), 8, 128), f32),
            pltpu.SemaphoreType.DMA((2, at_least(sends))),
            pltpu.SemaphoreType.DMA((2, dp)),
            pltpu.SemaphoreType.DMA((2, at_least(tallies))),
            pltpu.SemaphoreType.DMA,
        ],
        compiler_params=pltpu.CompilerParams(collective_id=2, has_side_effects=True),
        name="reduce_step",
    )(part, first_moment, second_moment)


def apply_kernel(basis_ref, update_ref, weight_ref, out_ref):
    tensor, _, width = basis_ref.shape
    delta = None
    for s in range(tensor):
        one = jnp.dot(
            basis_ref[s],
            update_ref[s * width : (s + 1) * width, :],
            preferred_element_type=jnp.float32,
        )
        delta = one if delta is None else delta + one
    kept = decay_keep * weight_ref[...].astype(jnp.float32)
    out_ref[...] = (kept - step_size * delta).astype(jnp.bfloat16)


def apply_update(basis, update, weight):
    rows, columns = weight.shape
    rank = update.shape[0]
    blocks = columns // 128
    tile = 128 * max(n for n in range(1, 9) if blocks % n == 0)
    return pl.pallas_call(
        apply_kernel,
        out_shape=jax.ShapeDtypeStruct(weight.shape, weight.dtype),
        grid=(columns // tile,),
        in_specs=[
            pl.BlockSpec(basis.shape, lambda n: (0, 0, 0)),
            pl.BlockSpec((rank, tile), lambda n: (0, n)),
            pl.BlockSpec((rows, tile), lambda n: (0, n)),
        ],
        out_specs=pl.BlockSpec((rows, tile), lambda n: (0, n)),
        name="apply_update",
    )(basis, update, weight)


def on_device(dp, tensor, inputs, out_grads, basis, weight, first_moment, second_moment):
    dims = factors(dp)
    per = dp // tensor
    pairs = []
    for d in range(dp):
        for t in range(tensor):
            target = (t * per + d % per) * tensor + d // per
            pairs.append((d * tensor + t, target))
    moved = lax.ppermute(basis, ("dp", "tensor"), pairs)
    gathered, back = gather_basis(moved, basis, dims, tensor)
    features = inputs.shape[1]
    grouped = gathered.reshape(tensor, features, basis.shape[1])
    projected = project(inputs, grouped, tensor)
    part = lax.dot_general(
        projected, out_grads, (((0,), (0,)), ((), ())), preferred_element_type=jnp.float32
    ).astype(jnp.bfloat16)
    rank, columns = part.shape
    bound_norm = math.sqrt(rank * columns * tensor)
    first, second, update = reduce_step(
        part.reshape(dp, rank // dp, columns), first_moment, second_moment, dims, tensor, bound_norm
    )
    new_weight = apply_update(back, update.reshape(rank, columns), weight)
    return (new_weight, first, second)


def solution(mesh):
    placed = P("dp", "tensor")
    return jax.shard_map(
        functools.partial(on_device, mesh.shape["dp"], mesh.shape["tensor"]),
        mesh=mesh,
        in_specs=(placed,) * 6,
        out_specs=(placed,) * 3,
        check_vma=False,
    )
```

```python
import functools
import math

import jax
import jax.numpy as jnp
from jax import lax
from jax.experimental import pallas as pl
from jax.experimental.pallas import tpu as pltpu
from jax.sharding import PartitionSpec as P

beta_one = 0.9
beta_two = 0.999
adam_eps = 1e-08
corr_one = 1.0 - 0.9**10
corr_two = 1.0 - 0.999**10
step_size = 0.002
decay_keep = 0.99

MESH = pl.DeviceIdType.MESH
ANY = pl.BlockSpec(memory_space=pl.ANY)
VMEM = pl.BlockSpec(memory_space=pltpu.VMEM)


def factors(dp):
    c = 2 if dp % 2 == 0 else 1
    y = 2 if (dp // c) % 2 == 0 else 1
    return dp // (c * y), y, c


class Place:
    def __init__(self, dims, tensor):
        self.dims, self.tensor = dims, tensor
        self.d = lax.axis_index("dp")
        _, ny, nc = dims
        self.z, self.y, self.c = self.d // (ny * nc), (self.d // nc) % ny, self.d % nc
        self.t = lax.axis_index("tensor")

    def unit(self, z, j=0, i=0):
        _, ny, nc = self.dims
        y = lax.rem(self.y + j + ny, ny) if j else self.y
        c = lax.rem(self.c + i + nc, nc) if i else self.c
        return (z * ny + y) * nc + c

    def peer(self, k=0, j=0, i=0, s=0):
        nz = self.dims[0]
        z = lax.rem(self.z + k + nz, nz) if k else self.z
        t = lax.rem(self.t + s, self.tensor) if s else self.t
        return (self.unit(z, j, i), t)

    def has(self, z):
        return jnp.logical_and(z >= 0, z < self.dims[0])

    def peers(self):
        nz, ny, nc = self.dims
        out = [self.peer(k=k) for k in range(1, nz)]
        out += [self.peer(j=j) for j in range(1, ny)]
        out += [self.peer(i=i) for i in range(1, nc)]
        out += [self.peer(s=s) for s in range(1, self.tensor)]
        return out


def greet(peers, extra=None):
    barrier = pltpu.get_barrier_semaphore()
    for p in peers:
        pl.semaphore_signal(barrier, inc=1, device_id=p, device_id_type=MESH)
    if extra is None:
        pl.semaphore_wait(barrier, len(peers))
        return

    @pl.when(extra[0])
    def _():
        pl.semaphore_signal(barrier, inc=1, device_id=extra[1], device_id_type=MESH)
        pl.semaphore_wait(barrier, len(peers) + 1)

    @pl.when(jnp.logical_not(extra[0]))
    def _():
        pl.semaphore_wait(barrier, len(peers))


def remote(src, dst, sems, slot, peer):
    return pltpu.make_async_remote_copy(
        src_ref=src,
        dst_ref=dst,
        send_sem=sems.at[0, slot],
        recv_sem=sems.at[1, slot],
        device_id=peer,
        device_id_type=MESH,
    )


def send(src, dst, sems, slot, peer):
    copy = remote(src, dst, sems, slot, peer)
    copy.start()
    return copy


def gather_slots(dims):
    nz, ny, nc = dims
    entries = 2 * (nz - 1) + 1
    return 2 * (nz - 1) + entries * (ny - 1) + entries * ny * (nc - 1)


def gather(at, own, full, sems, visit=lambda unit, ref: None):
    nz, ny, nc = at.dims
    entries = [(0, 0)] + [(h, way) for h in range(1, nz) for way in (1, -1)]
    hops = {e: n for n, e in enumerate(entries[1:])}
    slot = len(hops)
    sides, cores = {}, {}
    for e in entries:
        for j in range(1, ny):
            sides[e, j] = slot
            slot += 1
    for e in entries:
        for j in range(ny):
            for i in range(1, nc):
                cores[e, j, i] = slot
                slot += 1

    def source(e, j=0):
        h, way = e
        z = at.z - way * h
        if h == 0 and j == 0:
            return own, at.unit(z)
        u = at.unit(z, -j)
        return full.at[u], u

    def guarded(e, body):
        if e[0] == 0:
            body()
        else:
            pl.when(at.has(at.z - e[1] * e[0]))(body)

    def hop(e):
        h, way = e
        src, u = source((h - 1, way))
        return remote(src, full.at[u], sems, hops[e], at.peer(k=way))

    def side(e, j):
        src, u = source(e)
        return remote(src, full.at[u], sems, sides[e, j], at.peer(j=j))

    def core(e, j, i):
        src, u = source(e, j)
        return remote(src, full.at[u], sems, cores[e, j, i], at.peer(i=i))

    def pass_on(e):
        h, way = e
        for onward in (1, -1) if h == 0 else (way,):
            if h + 1 < nz:

                @pl.when(at.has(at.z + onward))
                def _():
                    hop((h + 1, onward)).start()

        for j in range(1, ny):
            side(e, j).start()
        for i in range(1, nc):
            core(e, 0, i).start()
        src, u = source(e)
        visit(u, src)

    def from_side(e):
        for j in range(1, ny):
            side(e, j).wait_recv()
            for i in range(1, nc):
                core(e, j, i).start()
            src, u = source(e, j)
            visit(u, src)

    def from_core(e):
        for j in range(ny):
            for i in range(1, nc):
                core(e, j, i).wait_recv()
                u = at.unit(at.z - e[1] * e[0], -j, -i)
                visit(u, full.at[u])

    pass_on((0, 0))
    for e in entries[1:]:

        def arrived(e=e):
            hop(e).wait_recv()
            pass_on(e)

        guarded(e, arrived)
    for e in entries:
        guarded(e, functools.partial(from_side, e))
    for e in entries:
        guarded(e, functools.partial(from_core, e))

    def drain(e):
        for j in range(1, ny):
            side(e, j).wait_send()
        for j in range(ny):
            for i in range(1, nc):
                core(e, j, i).wait_send()

    for e in entries:
        guarded(e, functools.partial(drain, e))
    for h, way in entries[1:]:

        @pl.when(jnp.logical_and(at.has(at.z + way), at.has(at.z - way * (h - 1))))
        def _():
            hop((h, way)).wait_send()


def project_kernel(
    dims, tensor, in_ref, basis_ref, out_ref, back,
    rows_in, own, full, acc, sent, got, sems, gather_sems, local,
):
    at = Place(dims, tensor)
    dp = math.prod(dims)
    per = dp // tensor
    swaps = at.t != at.d // per
    partner = (at.t * per + at.d % per, at.d // per)
    load = pltpu.make_async_copy(in_ref, rows_in, local.at[0])
    mine = pltpu.make_async_copy(basis_ref, own, local.at[1])
    mine_back = pltpu.make_async_copy(basis_ref, back.at[at.t], local.at[2])
    greet(at.peers(), (swaps, partner))
    swap = remote(basis_ref, own, sems, 0, partner)

    @pl.when(swaps)
    def _():
        swap.start()

    @pl.when(jnp.logical_not(swaps))
    def _():
        mine.start()

    load.start()
    mine_back.start()
    backs = [
        send(basis_ref, back.at[at.t], sems, s, at.peer(s=s)) for s in range(1, tensor)
    ]
    acc[...] = jnp.zeros_like(acc)
    load.wait()

    @pl.when(swaps)
    def _():
        swap.wait()

    @pl.when(jnp.logical_not(swaps))
    def _():
        mine.wait()

    depth, width = own.shape

    def visit(unit, ref):
        columns = pl.ds(pl.multiple_of((unit % per) * depth, depth), depth)
        acc[unit // per] += jnp.dot(
            rows_in[:, columns], ref[...], preferred_element_type=jnp.float32
        )

    gather(at, own, full, gather_sems, visit)

    copies = []
    for h in range(tensor):
        sent[h] = acc[h].astype(jnp.bfloat16)
        for s in range(1, tensor):
            copies.append(
                send(
                    sent.at[h],
                    got.at[s - 1, h],
                    sems,
                    tensor + h * (tensor - 1) + s - 1,
                    at.peer(s=s),
                )
            )
    for h in range(tensor):
        total = acc[h]
        for s in range(1, tensor):
            copies[h * (tensor - 1) + s - 1].wait_recv()
            total = total + got[s - 1, h].astype(jnp.float32)
        out_ref[:, h * width : (h + 1) * width] = total.astype(jnp.bfloat16)
    for copy in copies:
        copy.wait_send()
    for copy in backs:
        copy.wait()
    mine_back.wait()


def project(inputs, basis, dims, tensor):
    dp = math.prod(dims)
    tokens = inputs.shape[0]
    depth, width = basis.shape
    bf16 = jnp.bfloat16
    others = max(tensor - 1, 1)
    return pl.pallas_call(
        functools.partial(project_kernel, dims, tensor),
        out_shape=(
            jax.ShapeDtypeStruct((tokens, width * tensor), bf16),
            jax.ShapeDtypeStruct((tensor, depth, width), bf16),
        ),
        in_specs=[ANY, VMEM],
        out_specs=(VMEM, ANY),
        scratch_shapes=[
            pltpu.VMEM(inputs.shape, bf16),
            pltpu.VMEM((depth, width), bf16),
            pltpu.VMEM((dp, depth, width), bf16),
            pltpu.VMEM((tensor, tokens, width), jnp.float32),
            pltpu.VMEM((tensor, tokens, width), bf16),
            pltpu.VMEM((others, tensor, tokens, width), bf16),
            pltpu.SemaphoreType.DMA((2, tensor + tensor * others)),
            pltpu.SemaphoreType.DMA((2, max(gather_slots(dims), 1))),
            pltpu.SemaphoreType.DMA((3,)),
        ],
        compiler_params=pltpu.CompilerParams(collective_id=0, has_side_effects=True),
        name="project",
    )(inputs, basis)


def step_kernel(
    dims, tensor, bound_norm, part, m_ref, v_ref,
    first_ref, second_ref, full,
    r1, r2, r3, s1, s2, keep, upd, norm, sems, gather_sems, norm_sems, local,
):
    at = Place(dims, tensor)
    nz, ny, nc = dims
    f32 = jnp.float32
    greet(at.peers())

    entries = [(h, way) for h in range(nz - 1, 0, -1) for way in (1, -1)] + [(0, 0)]
    index = {e: n for n, e in enumerate(entries)}
    count = len(entries)

    def guarded(e, body):
        if e[0] == 0:
            body()
        else:
            pl.when(at.has(at.z + e[1] * e[0]))(body)

    def over_core(e, j, i):
        n = index[e]
        src = part.at[at.unit(at.z + e[1] * e[0], j, i)]
        slot = (n * ny + j) * (nc - 1) + i - 1
        return remote(src, r1.at[n, j, i - 1], sems, slot, at.peer(i=i))

    side_base = count * ny * (nc - 1)

    def over_side(e, j):
        n = index[e]
        slot = side_base + n * (ny - 1) + j - 1
        return remote(s1.at[n, j - 1], r2.at[n, j - 1], sems, slot, at.peer(j=j))

    line_base = side_base + count * (ny - 1)

    def over_line(h, way):
        line = 0 if way == 1 else 1
        slot = line_base + (h - 1) * 2 + line
        n = index[h, way]
        return remote(s2.at[n], r3.at[line, h - 1], sems, slot, at.peer(k=way))

    def start_cores(e):
        for j in [*range(1, ny), 0]:
            for i in range(1, nc):
                over_core(e, j, i).start()

    def core_sum(e, j):
        n = index[e]
        total = part[at.unit(at.z + e[1] * e[0], j)].astype(f32)
        for i in range(1, nc):
            over_core(e, j, i).wait_recv()
            total = total + r1[n, j, i - 1].astype(f32)
        return total

    def start_sides(e):
        n = index[e]
        for j in range(1, ny):
            s1[n, j - 1] = core_sum(e, j).astype(jnp.bfloat16)
            over_side(e, j).start()
        keep[n] = core_sum(e, 0)

    def arrive(e, way):
        line = 0 if way == 1 else 1
        over_line(e[0] + 1, way).wait_recv()
        keep[index[e]] += r3[line, e[0]].astype(f32)

    def start_line(e):
        n = index[e]
        for j in range(1, ny):
            over_side(e, j).wait_recv()
            keep[n] += r2[n, j - 1].astype(f32)
        for way in (1, -1) if e[0] == 0 else (e[1],):
            if e[0] + 1 < nz:
                pl.when(at.has(at.z - way))(functools.partial(arrive, e, way))
        if e[0]:
            s2[n] = keep[n].astype(jnp.bfloat16)
            over_line(*e).start()

    for stage in (start_cores, start_sides, start_line):
        for e in entries:
            guarded(e, functools.partial(stage, e))
    last = index[0, 0]
    total = keep[last]

    lanes = norm.shape[-1]
    columns = total.shape[1]
    squares = jnp.sum(total * total, axis=0, keepdims=True)
    folded = squares[:, :lanes]
    for a in range(1, columns // lanes):
        folded = folded + squares[:, a * lanes : (a + 1) * lanes]
    tally = jnp.broadcast_to(folded, (8, lanes))
    norm_copies, place = [], 0
    for number, axis in ((nc, "i"), (ny, "j"), (tensor, "s"), (nz, "k")):
        if number == 1:
            continue
        base = place
        norm[base] = tally
        copies = []
        for step in range(1, number):
            copies.append(
                send(norm.at[base], norm.at[base + step], norm_sems, base + step, at.peer(**{axis: step}))
            )
        for step in range(1, number):
            copies[step - 1].wait_recv()
            tally = tally + norm[base + step]
        norm_copies += copies
        place += number
    square = jnp.sum(tally[0:1, :], axis=1, keepdims=True)

    factor = jnp.minimum(1.0, bound_norm / (jnp.sqrt(square) + 1e-06))
    clipped = keep[last] * factor
    first = beta_one * m_ref[...] + (1.0 - beta_one) * clipped
    second = beta_two * v_ref[...] + (1.0 - beta_two) * clipped * clipped
    first_ref[...] = first
    second_ref[...] = second
    upd[...] = (first / corr_one / (jnp.sqrt(second / corr_two) + adam_eps)).astype(jnp.bfloat16)

    mine = pltpu.make_async_copy(upd, full.at[at.unit(at.z)], local)
    mine.start()
    gather(at, upd, full, gather_sems)
    mine.wait()

    def drain(e):
        for j in range(ny):
            for i in range(1, nc):
                over_core(e, j, i).wait_send()
            if j:
                over_side(e, j).wait_send()
        if e[0]:
            over_line(*e).wait_send()

    for e in entries:
        guarded(e, functools.partial(drain, e))
    for copy in norm_copies:
        copy.wait_send()


def reduce_step(part, first_moment, second_moment, dims, tensor, bound_norm):
    dp, rows, columns = part.shape
    nz, ny, nc = dims
    bf16, f32 = jnp.bfloat16, jnp.float32
    count = 2 * (nz - 1) + 1
    sends = count * (ny * (nc - 1) + ny - 1) + 2 * (nz - 1)
    tallies = sum(n for n in (nz, ny, nc, tensor) if n > 1)
    at_least = lambda n: max(n, 1)
    return pl.pallas_call(
        functools.partial(step_kernel, dims, tensor, bound_norm),
        out_shape=(
            jax.ShapeDtypeStruct((rows, columns), f32),
            jax.ShapeDtypeStruct((rows, columns), f32),
            jax.ShapeDtypeStruct((dp, rows, columns), bf16),
        ),
        in_specs=[VMEM, VMEM, VMEM],
        out_specs=(VMEM, VMEM, ANY),
        scratch_shapes=[
            pltpu.VMEM((count, ny, at_least(nc - 1), rows, columns), bf16),
            pltpu.VMEM((count, at_least(ny - 1), rows, columns), bf16),
            pltpu.VMEM((2, at_least(nz - 1), rows, columns), bf16),
            pltpu.VMEM((count, at_least(ny - 1), rows, columns), bf16),
            pltpu.VMEM((count, rows, columns), bf16),
            pltpu.VMEM((count, rows, columns), f32),
            pltpu.VMEM((rows, columns), bf16),
            pltpu.VMEM((at_least(tallies), 8, 128), f32),
            pltpu.SemaphoreType.DMA((2, at_least(sends))),
            pltpu.SemaphoreType.DMA((2, at_least(gather_slots(dims)))),
            pltpu.SemaphoreType.DMA((2, at_least(tallies))),
            pltpu.SemaphoreType.DMA,
        ],
        compiler_params=pltpu.CompilerParams(collective_id=1, has_side_effects=True),
        name="reduce_step",
    )(part, first_moment, second_moment)


def apply_kernel(basis_ref, update_ref, weight_ref, out_ref):
    tensor, _, width = basis_ref.shape
    delta = None
    for s in range(tensor):
        one = jnp.dot(
            basis_ref[s],
            update_ref[s * width : (s + 1) * width, :],
            preferred_element_type=jnp.float32,
        )
        delta = one if delta is None else delta + one
    kept = decay_keep * weight_ref[...].astype(jnp.float32)
    out_ref[...] = (kept - step_size * delta).astype(jnp.bfloat16)


def apply_update(basis, update, weight):
    rows, columns = weight.shape
    rank = update.shape[0]
    blocks = columns // 128
    tile = 128 * max(n for n in range(1, 9) if blocks % n == 0)
    return pl.pallas_call(
        apply_kernel,
        out_shape=jax.ShapeDtypeStruct(weight.shape, weight.dtype),
        grid=(columns // tile,),
        in_specs=[
            pl.BlockSpec(basis.shape, lambda n: (0, 0, 0)),
            pl.BlockSpec((rank, tile), lambda n: (0, n)),
            pl.BlockSpec((rows, tile), lambda n: (0, n)),
        ],
        out_specs=pl.BlockSpec((rows, tile), lambda n: (0, n)),
        name="apply_update",
    )(basis, update, weight)


def on_device(dp, tensor, inputs, out_grads, basis, weight, first_moment, second_moment):
    dims = factors(dp)
    projected, back = project(inputs, basis, dims, tensor)
    part = lax.dot_general(
        projected, out_grads, (((0,), (0,)), ((), ())), preferred_element_type=jnp.float32
    ).astype(jnp.bfloat16)
    rank, columns = part.shape
    bound_norm = math.sqrt(rank * columns * tensor)
    first, second, update = reduce_step(
        part.reshape(dp, rank // dp, columns), first_moment, second_moment, dims, tensor, bound_norm
    )
    new_weight = apply_update(back, update.reshape(rank, columns), weight)
    return (new_weight, first, second)


def solution(mesh):
    placed = P("dp", "tensor")
    return jax.shard_map(
        functools.partial(on_device, mesh.shape["dp"], mesh.shape["tensor"]),
        mesh=mesh,
        in_specs=(placed,) * 6,
        out_specs=(placed,) * 3,
        check_vma=False,
    )
```
